32 devices in a mesh: prow: 4 (over y, x), pcol: 8 (over z, core).
Axes of the slice: x: 2, y: 2, z: 4, core: 2. Of those that a mesh axis runs over, the one named last changes fastest.
Arguments:
- rhs: bfloat16 [3, 8, 512, 128], P(None, 'pcol', 'prow'), may hold values from -6 to 6
- inverse_diagonal_blocks: bfloat16 [3, 8, 512, 512], P(None, 'pcol'), may hold values from -1 to 2, as said below
- offdiagonal_blocks: bfloat16 [2, 8, 4, 512, 512], P(None, 'pcol', 'prow'), may hold values from -0.09375 to 0.09375
- targets: int32 [2, 8, 4], P(None, 'pcol'), may hold values from 0 to 15, as said below
Outputs:
- solution: bfloat16 [3, 8, 512, 128], P(None, 'pcol', 'prow')
The draws below stay inside these ranges and needn't reach their ends.
Inputs may be any that keep to these rules, and one draw needn't show every extreme that they name: For a supernode of level l the 4 entries of targets[l] are distinct and lie between l * 8 and (2) * 8 - 1, so they name supernodes of later levels only. Each block of inverse_diagonal_blocks is lower triangular.
All inputs are finite; a program needn't handle non-finite values.
Results may differ from the reference program's by a relative error of at most 0.014.
Values may be sent and summed in bfloat16 or wider, within the bound.
No kernel may reach another device: no remote copies, remote signals or barrier semaphores. Data moves between devices by JAX's collectives and lax.ppermute only.
A program may use at most 64 MiB of HBM per device.

```python
import math
import jax
import jax.numpy as jnp
from jax import lax

BLOCK = 512
VECTORS = 128
LEVELS = 3
OFF_COUNT = 4
LEVEL_SIZE = 8


def draw_inverse_diagonal_blocks(key, part):
    key_noise, key_diag = jax.random.split(jax.random.fold_in(key, 11))
    shape = (LEVELS, LEVEL_SIZE, BLOCK, BLOCK)
    noise = jnp.clip(jax.random.normal(key_noise, shape, jnp.float32), -4.0, 4.0)
    lower = jnp.tril(jnp.ones((BLOCK, BLOCK), jnp.float32), -1)
    diagonal = jax.random.uniform(key_diag, (LEVELS, LEVEL_SIZE, BLOCK), jnp.float32, 0.5, 2.0)
    identity_block = jnp.eye(BLOCK, dtype=jnp.float32)
    result = noise * lower * (0.7 / math.sqrt(BLOCK)) + diagonal[..., None] * identity_block
    return result.astype(jnp.bfloat16)


def draw_targets(key, part):
    stacked = []
    for present_level in range(LEVELS - 1):
        span_size = (LEVELS - 1 - present_level) * LEVEL_SIZE
        column_keys = jax.random.split(jax.random.fold_in(key, 101 + present_level), LEVEL_SIZE)
        orders = jax.vmap(lambda single: jax.random.permutation(single, span_size))(column_keys)
        stacked.append(orders[:, :OFF_COUNT].astype(jnp.int32) + present_level * LEVEL_SIZE)
    return jnp.stack(stacked).astype(jnp.int32)


def shard_levels(rng, dims, pieces, least, largest):
    gain = 1.0
    for axis_at, blocks in pieces:
        draws = jax.random.uniform(jax.random.fold_in(jax.random.fold_in(rng, 6), axis_at), (blocks,), jnp.float32, least / len(pieces), largest / len(pieces))
        gain = gain * jnp.repeat(jnp.exp(draws), dims[axis_at] // blocks).reshape((-1,) + (1,) * (len(dims) - 1 - axis_at))
    return gain


def bell_draw(stream_key, shape, deviation, limit, shards=(), held_as=jnp.bfloat16):
    array = deviation * jax.random.normal(stream_key, shape, jnp.float32)
    if shards:
        array = array * shard_levels(stream_key, shape, shards, -0.22, 0.18)
    return jnp.clip(array, -limit, limit).astype(held_as)


def setup_inputs(seed: int = 0) -> dict:
    streams_of = jax.random.split(jax.random.key(seed), 5)
    return {
        "rhs": bell_draw(streams_of[0], (LEVELS, LEVEL_SIZE, BLOCK, VECTORS), 1.0, 6.0, ((1, 8), (2, 4))),
        "inverse_diagonal_blocks": draw_inverse_diagonal_blocks(jax.random.fold_in(streams_of[4], 71), 0),
        "offdiagonal_blocks": bell_draw(streams_of[2], (LEVELS - 1, LEVEL_SIZE, OFF_COUNT, BLOCK, BLOCK), (2 * OFF_COUNT * BLOCK) ** -0.5, 0.09375, ((1, 8), (2, 4))),
        "targets": draw_targets(jax.random.fold_in(streams_of[4], 71), 0),
    }


def reference(rhs, inverse_diagonal_blocks, offdiagonal_blocks, targets):
    levels = rhs.shape[0]
    level_size = rhs.shape[1]
    upper_count = levels - 1
    updates = jnp.zeros((upper_count * level_size, BLOCK, VECTORS), jnp.float32)
    results = []
    for present_level in range(levels):
        remaining_rhs = rhs[present_level].astype(jnp.float32)
        if present_level > 0:
            remaining_rhs = remaining_rhs - updates[(present_level - 1) * level_size:present_level * level_size]
        finished_unknowns = jnp.einsum("rqe,rei->rqi", inverse_diagonal_blocks[present_level].astype(jnp.float32), remaining_rhs,
                            precision=lax.Precision.HIGHEST).astype(jnp.bfloat16)
        results.append(finished_unknowns)
        if present_level < upper_count:
            def add_column(running, column):
                blocks, chosen, vectors = column
                products = jnp.einsum("jab,bn->jan", blocks.astype(jnp.float32), vectors.astype(jnp.float32),
                                      precision=lax.Precision.HIGHEST)
                return running.at[chosen].add(products), None

            updates, _ = lax.scan(add_column, updates, (offdiagonal_blocks[present_level], targets[present_level], finished_unknowns))
    return jnp.stack(results)
```

```python
import functools

import jax
import jax.numpy as jnp
from jax import lax
from jax.experimental import pallas as pl
from jax.experimental.pallas import tpu as pltpu
from jax.sharding import PartitionSpec as P


F32 = jnp.float32
BF16 = jnp.bfloat16
NT = (((1,), (1,)), ((), ()))


def pairs(size, step):
    return [(i, i ^ step) for i in range(size)]


def call(kernel, out_shapes, operands, scalars=0, scratch=(), flops=0):
    vmem = pl.BlockSpec(memory_space=pltpu.VMEM)
    smem = pl.BlockSpec(memory_space=pltpu.SMEM)
    moved = sum(x.size * x.dtype.itemsize for x in operands)
    return pl.pallas_call(
        kernel,
        out_shape=out_shapes,
        in_specs=[smem] * scalars + [vmem] * (len(operands) - scalars),
        out_specs=[vmem] * len(out_shapes),
        scratch_shapes=list(scratch),
        cost_estimate=pl.CostEstimate(flops=flops, bytes_accessed=moved, transcendentals=0),
    )(*operands)


def first_kernel(rows, later, *refs):
    shares = refs[:rows]
    rest, inverse, block, kept = refs[rows : rows + 4]
    messages = refs[rows + 4 : 2 * rows + 4]
    whole, turned, turned_rest = refs[2 * rows + 4 :]
    part, vectors = shares[0].shape
    size = inverse.shape[0]
    each = vectors // rows
    me = lax.axis_index("prow")
    for step in range(rows):
        whole[pl.ds(pl.multiple_of((me ^ step) * part, part), part), :] = shares[step][...]
    solved = jnp.dot(inverse[...], whole[...], preferred_element_type=F32).astype(BF16)
    whole[...] = solved
    kept[...] = whole[pl.ds(pl.multiple_of(me * part, part), part), :]
    product = jnp.dot(block[...], solved, preferred_element_type=F32)
    turned[...] = product.T
    for level in range(later):
        turned_rest[level] = rest[level].astype(F32).T
    for step in range(rows):
        at = pl.ds(pl.multiple_of((me ^ step) * each, each), each)
        messages[step][:, :size] = turned[at, :].astype(BF16)
        for level in range(later):
            low = size + level * part
            messages[step][:, low : low + part] = turned_rest[level, at, :].astype(BF16)


def slots_kernel(rows, half, level, sources, own_targets, far_targets, *refs):
    own = refs[: len(sources)]
    far = refs[len(sources) : 2 * len(sources)]
    outs = refs[2 * len(sources) :]
    each, size = outs[0].shape
    me_row = lax.axis_index("prow")
    me_col = lax.axis_index("pcol")
    for step in range(half):
        column = (me_col ^ (2 * step)) + level * 2 * half
        total = jnp.zeros((each, size), F32)
        for targets, group in ((own_targets, own), (far_targets, far)):
            for (source, at), ref in zip(sources, group):
                value = ref[at] if ref.ndim == 3 else ref[:, :size]
                hit = targets[source[0], 0, me_row ^ source[1]] == column
                total = total + jnp.where(hit, value.astype(F32), 0.0)
        outs[step][...] = total.astype(outs[step].dtype)


def residual(rows, half, level, messages, arrived, out):
    each, size = out.shape
    part = size // rows
    me = lax.axis_index("prow")
    total = arrived[0][...].astype(F32)
    for ref in arrived[1:]:
        total = total + ref[...].astype(F32)
    low = size + level * part
    if part % 128 == 0:
        for step in range(rows):
            at = pl.ds(pl.multiple_of((me ^ step) * part, part), part)
            out[:, at] = messages[step][:, low : low + part].astype(F32)
        return out[...] - total
    given = jnp.zeros((each, size), F32)
    for step in range(rows):
        place = lax.broadcasted_iota(jnp.int32, (part, size), 1) - (me ^ step) * part
        chosen = (place == lax.broadcasted_iota(jnp.int32, (part, size), 0)).astype(F32).astype(BF16)
        given = given + jnp.dot(messages[step][:, low : low + part], chosen, preferred_element_type=F32)
    return given - total


def solve(inverse, given):
    high = given.astype(BF16)
    low = (given - high.astype(F32)).astype(BF16)
    both = jnp.concatenate([high, low], axis=0)
    wide = lax.dot_general(both, inverse[...], NT, preferred_element_type=F32)
    each = given.shape[0]
    return (wide[:each] + wide[each:]).astype(BF16)


def middle_kernel(rows, half, level, *refs):
    messages = refs[:rows]
    arrived = refs[rows : rows + half]
    inverse = refs[rows + half]
    blocks = refs[rows + half + 1 : 2 * rows + half + 1]
    solved, products, scratch = refs[2 * rows + half + 1 :]
    given = residual(rows, half, level - 1, messages, arrived, scratch)
    value = solve(inverse, given)
    solved[...] = value
    for step in range(rows):
        products[step] = lax.dot_general(value, blocks[step][...], NT, preferred_element_type=F32).astype(BF16)


def last_kernel(rows, half, level, before, *refs):
    messages = refs[:rows]
    arrived = refs[rows : rows + half]
    inverse = refs[rows + half]
    earlier = refs[rows + half + 1 : rows + half + 1 + before]
    outs = refs[rows + half + 1 + before : 2 * rows + half + 1 + before]
    scratch = refs[-1]
    each, size = scratch.shape
    part = size // rows
    me = lax.axis_index("prow")
    given = residual(rows, half, level - 1, messages, arrived, scratch)
    values = [ref[...] for ref in earlier] + [solve(inverse, given)]
    for index, value in enumerate(values):
        if part % 128 == 0:
            scratch[...] = value.astype(F32)
            for step in range(rows):
                at = pl.ds(pl.multiple_of((me ^ step) * part, part), part)
                outs[step][index] = scratch[:, at].astype(BF16)
        else:
            for step in range(rows):
                place = lax.broadcasted_iota(jnp.int32, (part, size), 1) - (me ^ step) * part
                chosen = (place == lax.broadcasted_iota(jnp.int32, (part, size), 0)).astype(F32).astype(BF16)
                outs[step][index] = lax.dot_general(value, chosen, NT, preferred_element_type=F32).astype(BF16)


def output_kernel(rows, later, *refs):
    kept = refs[0]
    pieces = refs[1 : rows + 1]
    out, scratch = refs[rows + 1 :]
    _, each, part = pieces[0].shape
    me = lax.axis_index("prow")
    out[0, 0] = kept[...]
    for level in range(later):
        for step in range(rows):
            at = pl.ds(pl.multiple_of((me ^ step) * each, each), each)
            scratch[at, :] = pieces[step][level].astype(F32)
        out[level + 1, 0] = scratch[...].T.astype(BF16)


def local(rhs, inverse, off, targets):
    levels, _, part, vectors = rhs.shape
    size = inverse.shape[-1]
    rows, columns = lax.axis_size("prow"), lax.axis_size("pcol")
    half = columns // 2
    later = levels - 1
    each = vectors // rows
    shape = jax.ShapeDtypeStruct

    def over_rows(x, step):
        return lax.ppermute(x, "prow", pairs(rows, step)) if step else x

    def over_pairs(x, step):
        return lax.ppermute(x, "pcol", pairs(columns, 2 * step)) if step else x

    def flip(x):
        return lax.ppermute(x, "pcol", pairs(columns, 1))

    far_targets = flip(targets)
    first = rhs[0, 0]
    shares = [over_rows(first, step) for step in range(rows)]
    width = size + later * part
    kept, *sent = call(
        functools.partial(first_kernel, rows, later),
        [shape((part, vectors), BF16)] + [shape((each, width), BF16)] * rows,
        [*shares, rhs[1:, 0], inverse[0, 0], off[0, 0, 0]],
        scratch=[pltpu.VMEM((size, vectors), BF16), pltpu.VMEM((vectors, size), F32), pltpu.VMEM((later, vectors, part), F32)],
        flops=4 * size * size * vectors,
    )
    messages = [over_rows(x, step) for step, x in enumerate(sent)]
    far_messages = [flip(x) for x in messages]
    blocks = {level: [over_rows(off[level, 0, 0], step) for step in range(rows)] for level in range(1, later)}

    own, far = list(messages), list(far_messages)
    sources = [((0, step), None) for step in range(rows)]
    solved = []
    for level in range(1, levels):
        out = call(
            functools.partial(slots_kernel, rows, half, level - 1, tuple(sources)),
            [shape((each, size), BF16)] * half,
            [targets, far_targets, *own, *far],
            scalars=2,
        )
        arrived = [over_pairs(x, step) for step, x in enumerate(out)]
        if level < later:
            value, products = call(
                functools.partial(middle_kernel, rows, half, level),
                [shape((each, size), BF16), shape((rows, each, size), BF16)],
                [*messages, *arrived, inverse[level, 0], *blocks[level]],
                scratch=[pltpu.VMEM((each, size), F32)],
                flops=2 * each * size * size * (rows + 1),
            )
            solved.append(value)
            far_products = flip(products)
            own += [products] * rows
            far += [far_products] * rows
            sources += [((level, step), step) for step in range(rows)]
    pieces = call(
        functools.partial(last_kernel, rows, half, later, len(solved)),
        [shape((later, each, part), BF16)] * rows,
        [*messages, *arrived, inverse[later, 0], *solved],
        scratch=[pltpu.VMEM((each, size), F32)],
        flops=2 * each * size * size,
    )
    pieces = [over_rows(x, step) for step, x in enumerate(pieces)]
    (out,) = call(
        functools.partial(output_kernel, rows, later),
        [shape((levels, 1, part, vectors), BF16)],
        [kept, *pieces],
        scratch=[pltpu.VMEM((vectors, part), F32)],
    )
    return out


def solution(mesh):
    in_specs = (
        P(None, "pcol", "prow", None),
        P(None, "pcol", None, None),
        P(None, "pcol", "prow", None, None),
        P(None, "pcol", None),
    )
    out_specs = P(None, "pcol", "prow", None)
    return jax.shard_map(local, mesh=mesh, in_specs=in_specs, out_specs=out_specs, check_vma=False)
```

```python
import functools

import jax
import jax.numpy as jnp
from jax import lax
from jax.experimental import pallas as pl
from jax.experimental.pallas import tpu as pltpu
from jax.sharding import PartitionSpec as P


F32 = jnp.float32
BF16 = jnp.bfloat16
NT = (((1,), (1,)), ((), ()))
GRANT = 24 << 20


def pairs(size, step):
    return [(i, i ^ step) for i in range(size)]


def call(kernel, out_shapes, operands, scalars=0, placed=0, scratch=(), flops=0):
    vmem = pl.BlockSpec(memory_space=pltpu.VMEM)
    smem = pl.BlockSpec(memory_space=pltpu.SMEM)
    moved = sum(x.size * x.dtype.itemsize for x in operands)
    return pl.pallas_call(
        kernel,
        out_shape=out_shapes,
        in_specs=[smem] * scalars + [vmem] * (len(operands) - scalars - placed) + [pl.BlockSpec(memory_space=pl.ANY)] * placed,
        out_specs=[vmem] * len(out_shapes),
        scratch_shapes=list(scratch),
        compiler_params=pltpu.CompilerParams(vmem_limit_bytes=GRANT),
        cost_estimate=pl.CostEstimate(flops=flops, bytes_accessed=moved, transcendentals=0),
    )(*operands)


def first_kernel(rows, later, *refs):
    shares = refs[:rows]
    inverse, rhs, off, kept = refs[rows : rows + 4]
    messages = refs[rows + 4 : 2 * rows + 4]
    whole, turned, turned_rest, rest, block, arrived = refs[2 * rows + 4 :]
    block_copy = pltpu.make_async_copy(off.at[0, 0, 0], block, arrived.at[0])
    rest_copy = pltpu.make_async_copy(rhs.at[pl.ds(1, later), 0], rest, arrived.at[1])
    block_copy.start()
    rest_copy.start()
    part, vectors = shares[0].shape
    size = inverse.shape[-1]
    each = vectors // rows
    me = lax.axis_index("prow")
    for step in range(rows):
        whole[pl.ds(pl.multiple_of((me ^ step) * part, part), part), :] = shares[step][...]
    solved = jnp.dot(inverse[...], whole[...], preferred_element_type=F32).astype(BF16)
    whole[...] = solved
    kept[...] = whole[pl.ds(pl.multiple_of(me * part, part), part), :]
    block_copy.wait()
    product = jnp.dot(block[...], solved, preferred_element_type=F32)
    turned[...] = product.T
    rest_copy.wait()
    for level in range(later):
        turned_rest[level] = rest[level].astype(F32).T
    for step in range(rows):
        at = pl.ds(pl.multiple_of((me ^ step) * each, each), each)
        messages[step][:, :size] = turned[at, :].astype(BF16)
        for level in range(later):
            low = size + level * part
            messages[step][:, low : low + part] = turned_rest[level, at, :].astype(BF16)


def slots_kernel(half, level, sources, own_targets, far_targets, *refs):
    own = refs[: len(sources)]
    far = refs[len(sources) : 2 * len(sources)]
    outs = refs[2 * len(sources) :]
    each, size = outs[0].shape
    me_row = lax.axis_index("prow")
    me_col = lax.axis_index("pcol")
    for step in range(half):
        column = (me_col ^ (2 * step)) + level * 2 * half
        total = jnp.zeros((each, size), F32)
        for targets, group in ((own_targets, own), (far_targets, far)):
            for (source, at), ref in zip(sources, group):
                value = ref[at] if ref.ndim == 3 else ref[:, :size]
                hit = targets[source[0], 0, me_row ^ source[1]] == column
                total = total + jnp.where(hit, value.astype(F32), 0.0)
        outs[step][...] = total.astype(outs[step].dtype)


def residual(rows, level, messages, arrived, out):
    each, size = out.shape
    part = size // rows
    me = lax.axis_index("prow")
    total = arrived[0][...].astype(F32)
    for ref in arrived[1:]:
        total = total + ref[...].astype(F32)
    low = size + level * part
    if part % 128 == 0:
        for step in range(rows):
            at = pl.ds(pl.multiple_of((me ^ step) * part, part), part)
            out[:, at] = messages[step][:, low : low + part].astype(F32)
        return out[...] - total
    given = jnp.zeros((each, size), F32)
    for step in range(rows):
        place = lax.broadcasted_iota(jnp.int32, (part, size), 1) - (me ^ step) * part
        chosen = (place == lax.broadcasted_iota(jnp.int32, (part, size), 0)).astype(F32).astype(BF16)
        given = given + jnp.dot(messages[step][:, low : low + part], chosen, preferred_element_type=F32)
    return given - total


def solve(inverse, level, given):
    high = given.astype(BF16)
    low = (given - high.astype(F32)).astype(BF16)
    both = jnp.concatenate([high, low], axis=0)
    wide = lax.dot_general(both, inverse[level, 0], NT, preferred_element_type=F32)
    each = given.shape[0]
    return (wide[:each] + wide[each:]).astype(BF16)


def middle_kernel(rows, half, level, *refs):
    messages = refs[:rows]
    arrived = refs[rows : rows + half]
    inverse = refs[rows + half]
    blocks = refs[rows + half + 1 : 3 * rows + half + 1]
    solved, products, scratch = refs[3 * rows + half + 1 :]
    given = residual(rows, level - 1, messages, arrived, scratch)
    value = solve(inverse, level, given)
    solved[...] = value
    for step in range(rows):
        low = 0
        for piece in blocks[2 * step : 2 * step + 2]:
            high = low + piece.shape[0]
            products[step, :, low:high] = lax.dot_general(value, piece[...], NT, preferred_element_type=F32).astype(BF16)
            low = high


def last_kernel(rows, half, level, before, *refs):
    messages = refs[:rows]
    arrived = refs[rows : rows + half]
    inverse = refs[rows + half]
    earlier = refs[rows + half + 1 : rows + half + 1 + before]
    outs = refs[rows + half + 1 + before : 2 * rows + half + 1 + before]
    scratch = refs[-1]
    _, size = scratch.shape
    part = size // rows
    me = lax.axis_index("prow")
    given = residual(rows, level - 1, messages, arrived, scratch)
    values = [ref[...] for ref in earlier] + [solve(inverse, level, given)]
    for index, value in enumerate(values):
        if part % 128 == 0:
            scratch[...] = value.astype(F32)
            for step in range(rows):
                at = pl.ds(pl.multiple_of((me ^ step) * part, part), part)
                outs[step][index] = scratch[:, at].astype(BF16)
        else:
            for step in range(rows):
                place = lax.broadcasted_iota(jnp.int32, (part, size), 1) - (me ^ step) * part
                chosen = (place == lax.broadcasted_iota(jnp.int32, (part, size), 0)).astype(F32).astype(BF16)
                outs[step][index] = lax.dot_general(value, chosen, NT, preferred_element_type=F32).astype(BF16)


def output_kernel(rows, later, *refs):
    kept = refs[0]
    pieces = refs[1 : rows + 1]
    out, scratch = refs[rows + 1 :]
    _, each, _ = pieces[0].shape
    me = lax.axis_index("prow")
    out[0, 0] = kept[...]
    for level in range(later):
        for step in range(rows):
            at = pl.ds(pl.multiple_of((me ^ step) * each, each), each)
            scratch[at, :] = pieces[step][level].astype(F32)
        out[level + 1, 0] = scratch[...].T.astype(BF16)


def local(rhs, inverse, off, targets):
    levels, _, part, vectors = rhs.shape
    size = inverse.shape[-1]
    rows, columns = lax.axis_size("prow"), lax.axis_size("pcol")
    half = columns // 2
    later = levels - 1
    each = vectors // rows
    shape = jax.ShapeDtypeStruct

    def over_rows(x, step):
        return lax.ppermute(x, "prow", pairs(rows, step)) if step else x

    def over_pairs(x, step):
        return lax.ppermute(x, "pcol", pairs(columns, 2 * step)) if step else x

    def flip(x):
        return lax.ppermute(x, "pcol", pairs(columns, 1))

    far_targets = flip(targets)
    first = rhs[0, 0]
    shares = [over_rows(first, step) for step in range(rows)]
    width = size + later * part
    kept, *sent = call(
        functools.partial(first_kernel, rows, later),
        [shape((part, vectors), BF16)] + [shape((each, width), BF16)] * rows,
        [*shares, inverse[0, 0], rhs, off],
        placed=2,
        scratch=[
            pltpu.VMEM((size, vectors), BF16),
            pltpu.VMEM((vectors, size), F32),
            pltpu.VMEM((later, vectors, part), F32),
            pltpu.VMEM((later, part, vectors), BF16),
            pltpu.VMEM((size, size), BF16),
            pltpu.SemaphoreType.DMA((2,)),
        ],
        flops=4 * size * size * vectors,
    )
    messages = [over_rows(x, step) for step, x in enumerate(sent)]
    far_messages = [flip(x) for x in messages]
    blocks = {}
    for level in range(1, later):
        cut = size // 2
        upper, lower = off[level, 0, 0, :cut], off[level, 0, 0, cut:]
        late_upper, late_lower, _ = lax.optimization_barrier((upper, lower, sent[0]))
        bits = [1 << b for b in range(rows.bit_length() - 1)]
        blocks[level] = [None] * (2 * rows)
        for side, (early, late, order) in enumerate(((upper, late_upper, bits), (lower, late_lower, bits[::-1]))):
            have = {0: early}
            for number, bit in enumerate(order):
                for step in sorted(have):
                    source = have[step]
                    if number:
                        source = late if step == 0 else lax.optimization_barrier((source, sent[0]))[0]
                    blocks[level][2 * (step ^ bit) + side] = over_rows(source, bit)
                have = {step: blocks[level][2 * step + side] if step else early for step in [*have, *(x ^ bit for x in have)]}
            blocks[level][side] = early

    own, far = list(messages), list(far_messages)
    sources = [((0, step), None) for step in range(rows)]
    solved = []
    for level in range(1, levels):
        out = call(
            functools.partial(slots_kernel, half, level - 1, tuple(sources)),
            [shape((each, size), BF16)] * half,
            [targets, far_targets, *own, *far],
            scalars=2,
        )
        arrived = [over_pairs(x, step) for step, x in enumerate(out)]
        if level < later:
            value, products = call(
                functools.partial(middle_kernel, rows, half, level),
                [shape((each, size), BF16), shape((rows, each, size), BF16)],
                [*messages, *arrived, inverse, *blocks[level]],
                scratch=[pltpu.VMEM((each, size), F32)],
                flops=2 * each * size * size * (rows + 1),
            )
            solved.append(value)
            far_products = flip(products)
            own += [products] * rows
            far += [far_products] * rows
            sources += [((level, step), step) for step in range(rows)]
    pieces = call(
        functools.partial(last_kernel, rows, half, later, len(solved)),
        [shape((later, each, part), BF16)] * rows,
        [*messages, *arrived, inverse, *solved],
        scratch=[pltpu.VMEM((each, size), F32)],
        flops=2 * each * size * size,
    )
    pieces = [over_rows(x, step) for step, x in enumerate(pieces)]
    (out,) = call(
        functools.partial(output_kernel, rows, later),
        [shape((levels, 1, part, vectors), BF16)],
        [kept, *pieces],
        scratch=[pltpu.VMEM((vectors, part), F32)],
    )
    return out


def solution(mesh):
    in_specs = (
        P(None, "pcol", "prow", None),
        P(None, "pcol", None, None),
        P(None, "pcol", "prow", None, None),
        P(None, "pcol", None),
    )
    out_specs = P(None, "pcol", "prow", None)

    return jax.shard_map(local, mesh=mesh, in_specs=in_specs, out_specs=out_specs, check_vma=False)
```

```python
import functools

import jax
import jax.numpy as jnp
from jax import lax
from jax.experimental import pallas as pl
from jax.experimental.pallas import tpu as pltpu
from jax.sharding import PartitionSpec as P


F32 = jnp.float32
BF16 = jnp.bfloat16
NT = (((1,), (1,)), ((), ()))
GRANT = 24 << 20


def pairs(size, step):
    return [(i, i ^ step) for i in range(size)]


def call(kernel, out_shapes, operands, scalars=0, placed=0, scratch=(), flops=0):
    vmem = pl.BlockSpec(memory_space=pltpu.VMEM)
    smem = pl.BlockSpec(memory_space=pltpu.SMEM)
    moved = sum(x.size * x.dtype.itemsize for x in operands)
    return pl.pallas_call(
        kernel,
        out_shape=out_shapes,
        in_specs=[smem] * scalars + [vmem] * (len(operands) - scalars - placed) + [pl.BlockSpec(memory_space=pltpu.HBM if placed == len(operands) else pl.ANY)] * placed,
        out_specs=[vmem] * len(out_shapes),
        scratch_shapes=list(scratch),
        compiler_params=pltpu.CompilerParams(vmem_limit_bytes=GRANT),
        cost_estimate=pl.CostEstimate(flops=flops, bytes_accessed=moved, transcendentals=0),
    )(*operands)


def load_kernel(later, rhs, inverse, off, first, *refs):
    blocks, top, done = refs[: later - 1], refs[later - 1], refs[later]
    copies = [(rhs.at[0, 0], first), (inverse.at[0, 0], top)]
    copies += [(off.at[level + 1, 0, 0], block) for level, block in enumerate(blocks)]
    copies = [pltpu.make_async_copy(*ends, done.at[at]) for at, ends in enumerate(copies)]
    for copy in copies:
        copy.start()
    for copy in copies:
        copy.wait()


def first_kernel(rows, later, *refs):
    shares = refs[:rows]
    inverse, rhs, off, kept = refs[rows : rows + 4]
    messages = refs[rows + 4 : 2 * rows + 4]
    whole, turned, turned_rest, rest, block, arrived = refs[2 * rows + 4 :]
    block_copy = pltpu.make_async_copy(off.at[0, 0, 0], block, arrived.at[0])
    rest_copy = pltpu.make_async_copy(rhs.at[pl.ds(1, later), 0], rest, arrived.at[1])
    block_copy.start()
    rest_copy.start()
    part, vectors = shares[0].shape
    size = inverse.shape[-1]
    each = vectors // rows
    me = lax.axis_index("prow")
    for step in range(rows):
        whole[pl.ds(pl.multiple_of((me ^ step) * part, part), part), :] = shares[step][...]
    solved = jnp.dot(inverse[...], whole[...], preferred_element_type=F32).astype(BF16)
    whole[...] = solved
    kept[...] = whole[pl.ds(pl.multiple_of(me * part, part), part), :]
    block_copy.wait()
    product = jnp.dot(block[...], solved, preferred_element_type=F32)
    turned[...] = product.T
    rest_copy.wait()
    for level in range(later):
        turned_rest[level] = rest[level].astype(F32).T
    for step in range(rows):
        at = pl.ds(pl.multiple_of((me ^ step) * each, each), each)
        messages[step][:, :size] = turned[at, :].astype(BF16)
        for level in range(later):
            low = size + level * part
            messages[step][:, low : low + part] = turned_rest[level, at, :].astype(BF16)


def slots_kernel(half, level, sources, own_targets, far_targets, *refs):
    own = refs[: len(sources)]
    far = refs[len(sources) : 2 * len(sources)]
    outs = refs[2 * len(sources) :]
    each, size = outs[0].shape
    me_row = lax.axis_index("prow")
    me_col = lax.axis_index("pcol")
    for step in range(half):
        column = (me_col ^ (2 * step)) + level * 2 * half
        total = jnp.zeros((each, size), F32)
        for targets, group, odd in ((own_targets, own, me_col % 2), (far_targets, far, 1 - me_col % 2)):
            for (source, turns, at), ref in zip(sources, group):
                value = ref[:, :size] if at is None else ref[at]
                turn = turns[0] if turns[0] == turns[1] else jnp.where(odd == 1, turns[1], turns[0])
                hit = targets[source, 0, me_row ^ turn] == column
                total = total + jnp.where(hit, value.astype(F32), 0.0)
        outs[step][...] = total.astype(outs[step].dtype)


def residual(rows, level, messages, arrived, out):
    each, size = out.shape
    part = size // rows
    me = lax.axis_index("prow")
    total = arrived[0][...].astype(F32)
    for ref in arrived[1:]:
        total = total + ref[...].astype(F32)
    low = size + level * part
    if part % 128 == 0:
        for step in range(rows):
            at = pl.ds(pl.multiple_of((me ^ step) * part, part), part)
            out[:, at] = messages[step][:, low : low + part].astype(F32)
        return out[...] - total
    given = jnp.zeros((each, size), F32)
    for step in range(rows):
        place = lax.broadcasted_iota(jnp.int32, (part, size), 1) - (me ^ step) * part
        chosen = (place == lax.broadcasted_iota(jnp.int32, (part, size), 0)).astype(F32).astype(BF16)
        given = given + jnp.dot(messages[step][:, low : low + part], chosen, preferred_element_type=F32)
    return given - total


def solve(inverse, level, given):
    high = given.astype(BF16)
    low = (given - high.astype(F32)).astype(BF16)
    both = jnp.concatenate([high, low], axis=0)
    wide = lax.dot_general(both, inverse[level, 0], NT, preferred_element_type=F32)
    each = given.shape[0]
    return (wide[:each] + wide[each:]).astype(BF16)


def middle_kernel(rows, half, level, *refs):
    messages = refs[:rows]
    arrived = refs[rows : rows + half]
    inverse = refs[rows + half]
    blocks = refs[rows + half + 1 : 2 * rows + half + 1]
    solved, products, scratch = refs[2 * rows + half + 1 :]
    given = residual(rows, level - 1, messages, arrived, scratch)
    value = solve(inverse, level, given)
    solved[...] = value
    for at, block in enumerate(blocks):
        products[at] = lax.dot_general(value, block[...], NT, preferred_element_type=F32).astype(BF16)


def last_kernel(rows, half, level, before, *refs):
    messages = refs[:rows]
    arrived = refs[rows : rows + half]
    inverse = refs[rows + half]
    earlier = refs[rows + half + 1 : rows + half + 1 + before]
    outs = refs[rows + half + 1 + before : 2 * rows + half + 1 + before]
    scratch = refs[-1]
    _, size = scratch.shape
    part = size // rows
    me = lax.axis_index("prow")
    given = residual(rows, level - 1, messages, arrived, scratch)
    values = [ref[...] for ref in earlier] + [solve(inverse, level, given)]
    for index, value in enumerate(values):
        if part % 128 == 0:
            scratch[...] = value.astype(F32)
            for step in range(rows):
                at = pl.ds(pl.multiple_of((me ^ step) * part, part), part)
                outs[step][index] = scratch[:, at].astype(BF16)
        else:
            for step in range(rows):
                place = lax.broadcasted_iota(jnp.int32, (part, size), 1) - (me ^ step) * part
                chosen = (place == lax.broadcasted_iota(jnp.int32, (part, size), 0)).astype(F32).astype(BF16)
                outs[step][index] = lax.dot_general(value, chosen, NT, preferred_element_type=F32).astype(BF16)


def output_kernel(rows, later, *refs):
    kept = refs[0]
    pieces = refs[1 : rows + 1]
    out, scratch = refs[rows + 1 :]
    _, each, _ = pieces[0].shape
    me = lax.axis_index("prow")
    out[0, 0] = kept[...]
    for level in range(later):
        for step in range(rows):
            at = pl.ds(pl.multiple_of((me ^ step) * each, each), each)
            scratch[at, :] = pieces[step][level].astype(F32)
        out[level + 1, 0] = scratch[...].T.astype(BF16)


def local(rhs, inverse, off, targets):
    levels, _, part, vectors = rhs.shape
    size = inverse.shape[-1]
    rows, columns = lax.axis_size("prow"), lax.axis_size("pcol")
    half = columns // 2
    later = levels - 1
    each = vectors // rows
    shape = jax.ShapeDtypeStruct

    def over_rows(x, step):
        return lax.ppermute(x, "prow", pairs(rows, step)) if step else x

    def over_turns(x, turn):
        links = [(r * columns + c, (r ^ turn[c % 2]) * columns + c) for r in range(rows) for c in range(columns)]
        return lax.ppermute(x, ("prow", "pcol"), links)

    def over_pairs(x, step):
        return lax.ppermute(x, "pcol", pairs(columns, 2 * step)) if step else x

    def flip(x):
        return lax.ppermute(x, "pcol", pairs(columns, 1))

    far_targets = flip(targets)
    first, *owned, top = call(
        functools.partial(load_kernel, later),
        [shape((part, vectors), BF16)] + [shape((size, size), BF16)] * later,
        [pltpu.with_memory_space_constraint(x, pltpu.HBM) for x in (rhs, inverse, off)],
        placed=3,
        scratch=[pltpu.SemaphoreType.DMA((later + 1,))],
    )
    shares = [over_rows(first, step) for step in range(rows)]
    width = size + later * part
    kept, *sent = call(
        functools.partial(first_kernel, rows, later),
        [shape((part, vectors), BF16)] + [shape((each, width), BF16)] * rows,
        [*shares, top, rhs, off],
        placed=2,
        scratch=[
            pltpu.VMEM((size, vectors), BF16),
            pltpu.VMEM((vectors, size), F32),
            pltpu.VMEM((later, vectors, part), F32),
            pltpu.VMEM((later, part, vectors), BF16),
            pltpu.VMEM((size, size), BF16),
            pltpu.SemaphoreType.DMA((2,)),
        ],
        flops=4 * size * size * vectors,
    )
    messages = [over_rows(x, step) for step, x in enumerate(sent)]
    far_messages = [flip(x) for x in messages]
    bits = [1 << b for b in range(rows.bit_length() - 1)]
    blocks, steps = {}, [(0, 0)]
    for level in range(1, later):
        have = [owned[level - 1]]
        for turn in zip(bits, bits[::-1]):
            have += [over_turns(x, turn) for x in have]
        blocks[level] = have
    for turn in zip(bits, bits[::-1]):
        steps += [(even ^ turn[0], odd ^ turn[1]) for even, odd in steps]

    own, far = list(messages), list(far_messages)
    sources = [(0, (step, step), None) for step in range(rows)]
    solved = []
    for level in range(1, levels):
        out = call(
            functools.partial(slots_kernel, half, level - 1, tuple(sources)),
            [shape((each, size), BF16)] * half,
            [targets, far_targets, *own, *far],
            scalars=2,
        )
        arrived = [over_pairs(x, step) for step, x in enumerate(out)]
        if level < later:
            value, products = call(
                functools.partial(middle_kernel, rows, half, level),
                [shape((each, size), BF16), shape((rows, each, size), BF16)],
                [*messages, *arrived, inverse, *blocks[level]],
                scratch=[pltpu.VMEM((each, size), F32)],
                flops=2 * each * size * size * (rows + 1),
            )
            solved.append(value)
            far_products = flip(products)
            own += [products] * rows
            far += [far_products] * rows
            sources += [(level, turns, at) for at, turns in enumerate(steps)]
    pieces = call(
        functools.partial(last_kernel, rows, half, later, len(solved)),
        [shape((later, each, part), BF16)] * rows,
        [*messages, *arrived, inverse, *solved],
        scratch=[pltpu.VMEM((each, size), F32)],
        flops=2 * each * size * size,
    )
    pieces = [over_rows(x, step) for step, x in enumerate(pieces)]
    (out,) = call(
        functools.partial(output_kernel, rows, later),
        [shape((levels, 1, part, vectors), BF16)],
        [kept, *pieces],
        scratch=[pltpu.VMEM((vectors, part), F32)],
    )
    return out


def solution(mesh):
    in_specs = (
        P(None, "pcol", "prow", None),
        P(None, "pcol", None, None),
        P(None, "pcol", "prow", None, None),
        P(None, "pcol", None),
    )
    out_specs = P(None, "pcol", "prow", None)

    return jax.shard_map(local, mesh=mesh, in_specs=in_specs, out_specs=out_specs, check_vma=False)
```

```python
import functools

import jax
import jax.numpy as jnp
from jax import lax
from jax.experimental import pallas as pl
from jax.experimental.pallas import tpu as pltpu
from jax.sharding import PartitionSpec as P


F32 = jnp.float32
BF16 = jnp.bfloat16
NT = (((1,), (1,)), ((), ()))
GRANT = 24 << 20


def pairs(size, step):
    return [(i, i ^ step) for i in range(size)]


def call(kernel, out_shapes, operands, scalars=0, placed=0, out_space=pltpu.VMEM, scratch=(), flops=0):
    vmem = pl.BlockSpec(memory_space=pltpu.VMEM)
    smem = pl.BlockSpec(memory_space=pltpu.SMEM)
    moved = sum(x.size * x.dtype.itemsize for x in operands)
    return pl.pallas_call(
        kernel,
        out_shape=out_shapes,
        in_specs=[smem] * scalars + [vmem] * (len(operands) - scalars - placed) + [pl.BlockSpec(memory_space=pltpu.HBM if placed == len(operands) else pl.ANY)] * placed,
        out_specs=[pl.BlockSpec(memory_space=out_space)] * len(out_shapes),
        scratch_shapes=list(scratch),
        compiler_params=pltpu.CompilerParams(vmem_limit_bytes=GRANT),
        cost_estimate=pl.CostEstimate(flops=flops, bytes_accessed=moved, transcendentals=0),
    )(*operands)


def load_kernel(places, *refs):
    done = refs[-1]
    outs = refs[len(refs) - 1 - len(places) : -1]
    copies = [pltpu.make_async_copy(refs[at].at[place], out, done.at[i]) for i, ((at, place), out) in enumerate(zip(places, outs))]
    for copy in copies:
        copy.start()
    for copy in copies:
        copy.wait()


def first_kernel(rows, later, *refs):
    shares = refs[:rows]
    inverse, rhs, off, kept = refs[rows : rows + 4]
    messages = refs[rows + 4 : 2 * rows + 4]
    whole, turned, turned_rest = refs[2 * rows + 4 :]
    part, vectors = shares[0].shape
    size = inverse.shape[-1]
    each = vectors // rows
    me = lax.axis_index("prow")
    for step in range(rows):
        whole[pl.ds(pl.multiple_of((me ^ step) * part, part), part), :] = shares[step][...]
    solved = jnp.dot(inverse[...], whole[...], preferred_element_type=F32).astype(BF16)
    whole[...] = solved
    kept[...] = whole[pl.ds(pl.multiple_of(me * part, part), part), :]
    product = jnp.dot(off[0, 0, 0], solved, preferred_element_type=F32)
    turned[...] = product.T
    for level in range(later):
        turned_rest[level] = rhs[level + 1, 0].astype(F32).T
    for step in range(rows):
        at = pl.ds(pl.multiple_of((me ^ step) * each, each), each)
        messages[step][:, :size] = turned[at, :].astype(BF16)
        for level in range(later):
            low = size + level * part
            messages[step][:, low : low + part] = turned_rest[level, at, :].astype(BF16)


def slot_of(targets, source, turns, odd, half, level):
    me_col = lax.axis_index("pcol")
    turn = turns[0] if turns[0] == turns[1] else jnp.where(odd == 1, turns[1], turns[0])
    column = targets[source, 0, lax.axis_index("prow") ^ turn] - level * 2 * half
    wanted = (column >= 0) & (column < 2 * half) & ((column & 1) == (me_col & 1))
    return wanted, (column >> 1) ^ (me_col >> 1)


def weights_kernel(half, level, turns, own_targets, far_targets, out):
    parity = lax.axis_index("pcol") & 1
    for group, (targets, odd) in enumerate(((own_targets, parity), (far_targets, 1 - parity))):
        for at, turn in enumerate(turns):
            wanted, slot = slot_of(targets, level, turn, odd, half, level)
            for step in range(half):
                value = jnp.where(wanted & (slot == step), 1.0, 0.0).astype(F32)
                out[group * len(turns) + at, step] = jnp.full(out.shape[2:], value, F32)


def earlier_kernel(half, level, sources, own_targets, far_targets, *refs):
    own = refs[: len(sources)]
    far = refs[len(sources) : 2 * len(sources)]
    total = refs[-1]
    size = total.shape[2]
    parity = lax.axis_index("pcol") & 1
    total[...] = jnp.zeros_like(total)

    def add(wanted, slot, at, ref):
        @pl.when(wanted)
        def _():
            value = ref[:, :size] if at is None else ref[at]
            total[slot] += value.astype(F32)

    for targets, group, odd in ((own_targets, own, parity), (far_targets, far, 1 - parity)):
        for (source, turns, at), ref in zip(sources, group):
            add(*slot_of(targets, source, turns, odd, half, level), at, ref)


def slots_kernel(half, places, weights, *refs):
    products = refs[: len(places)]
    outs = refs[-half:]
    before = refs[len(places) : -half]
    each, size = outs[0].shape
    chunk = min(16, each)
    for low in range(0, each, chunk):
        at_rows = pl.ds(low, chunk)
        totals = [before[0][step, at_rows, :] if before else jnp.zeros((chunk, size), F32) for step in range(half)]
        for number, (at, ref) in enumerate(zip(places, products)):
            value = (ref[at_rows, :size] if at is None else ref[at, at_rows, :]).astype(F32)
            for step in range(half):
                totals[step] = totals[step] + value * jnp.tile(weights[number, step], (chunk // 8, size // 128))
        for step in range(half):
            outs[step][at_rows, :] = totals[step].astype(outs[step].dtype)


def residual(rows, level, messages, arrived, out):
    each, size = out.shape
    part = size // rows
    me = lax.axis_index("prow")
    total = arrived[0][...].astype(F32)
    for ref in arrived[1:]:
        total = total + ref[...].astype(F32)
    low = size + level * part
    if part % 128 == 0:
        for step in range(rows):
            at = pl.ds(pl.multiple_of((me ^ step) * part, part), part)
            out[:, at] = messages[step][:, low : low + part].astype(F32)
        return out[...] - total
    given = jnp.zeros((each, size), F32)
    for step in range(rows):
        place = lax.broadcasted_iota(jnp.int32, (part, size), 1) - (me ^ step) * part
        chosen = (place == lax.broadcasted_iota(jnp.int32, (part, size), 0)).astype(F32).astype(BF16)
        given = given + jnp.dot(messages[step][:, low : low + part], chosen, preferred_element_type=F32)
    return given - total


def solve(inverse, level, given):
    high = given.astype(BF16)
    low = (given - high.astype(F32)).astype(BF16)
    both = jnp.concatenate([high, low], axis=0)
    wide = lax.dot_general(both, inverse[level, 0], NT, preferred_element_type=F32)
    each = given.shape[0]
    return (wide[:each] + wide[each:]).astype(BF16)


def middle_kernel(rows, half, level, *refs):
    messages = refs[:rows]
    arrived = refs[rows : rows + half]
    inverse = refs[rows + half]
    blocks = refs[rows + half + 1 : 2 * rows + half + 1]
    solved, products, scratch = refs[2 * rows + half + 1 :]
    given = residual(rows, level - 1, messages, arrived, scratch)
    value = solve(inverse, level, given)
    solved[...] = value
    for at, block in enumerate(blocks):
        products[at] = lax.dot_general(value, block[...], NT, preferred_element_type=F32).astype(BF16)


def last_kernel(rows, half, level, before, *refs):
    messages = refs[:rows]
    arrived = refs[rows : rows + half]
    inverse = refs[rows + half]
    earlier = refs[rows + half + 1 : rows + half + 1 + before]
    outs = refs[rows + half + 1 + before : 2 * rows + half + 1 + before]
    scratch = refs[-1]
    _, size = scratch.shape
    part = size // rows
    me = lax.axis_index("prow")
    given = residual(rows, level - 1, messages, arrived, scratch)
    values = [ref[...] for ref in earlier] + [solve(inverse, level, given)]
    for index, value in enumerate(values):
        if part % 128 == 0:
            scratch[...] = value.astype(F32)
            for step in range(rows):
                at = pl.ds(pl.multiple_of((me ^ step) * part, part), part)
                outs[step][index] = scratch[:, at].astype(BF16)
        else:
            for step in range(rows):
                place = lax.broadcasted_iota(jnp.int32, (part, size), 1) - (me ^ step) * part
                chosen = (place == lax.broadcasted_iota(jnp.int32, (part, size), 0)).astype(F32).astype(BF16)
                outs[step][index] = lax.dot_general(value, chosen, NT, preferred_element_type=F32).astype(BF16)


def output_kernel(rows, later, *refs):
    kept = refs[0]
    pieces = refs[1 : rows + 1]
    out, scratch, turned, done = refs[rows + 1 :]
    _, each, _ = pieces[0].shape
    me = lax.axis_index("prow")
    copies = [pltpu.make_async_copy(kept, out.at[0, 0], done.at[0])]
    copies[0].start()
    for level in range(later):
        for step in range(rows):
            at = pl.ds(pl.multiple_of((me ^ step) * each, each), each)
            scratch[level, at, :] = pieces[step][level].astype(F32)
        turned[level] = scratch[level].T.astype(BF16)
        copies.append(pltpu.make_async_copy(turned.at[level], out.at[level + 1, 0], done.at[level + 1]))
        copies[-1].start()
    for copy in copies:
        copy.wait()


def local(rhs, inverse, off, targets):
    levels, _, part, vectors = rhs.shape
    size = inverse.shape[-1]
    rows, columns = lax.axis_size("prow"), lax.axis_size("pcol")
    half = columns // 2
    later = levels - 1
    each = vectors // rows
    shape = jax.ShapeDtypeStruct

    def over_rows(x, step):
        return lax.ppermute(x, "prow", pairs(rows, step)) if step else x

    def over_turns(x, turn):
        links = [(r * columns + c, (r ^ turn[c % 2]) * columns + c) for r in range(rows) for c in range(columns)]
        return lax.ppermute(x, ("prow", "pcol"), links)

    def over_pairs(x, step):
        return lax.ppermute(x, "pcol", pairs(columns, 2 * step)) if step else x

    def flip(x):
        return lax.ppermute(x, "pcol", pairs(columns, 1))

    far_targets = flip(targets)

    def load(places, out_shapes, operands):
        return call(
            functools.partial(load_kernel, places),
            out_shapes,
            [pltpu.with_memory_space_constraint(x, pltpu.HBM) for x in operands],
            placed=len(operands),
            scratch=[pltpu.SemaphoreType.DMA((len(places),))],
        )

    first, *owned = load(
        [(0, (0, 0))] + [(1, (level, 0, 0)) for level in range(1, later)],
        [shape((part, vectors), BF16)] + [shape((size, size), BF16)] * (later - 1),
        [rhs, off],
    )
    (top,) = load([(0, (0, 0))], [shape((size, size), BF16)], [inverse])
    shares = [over_rows(first, step) for step in range(rows)]
    width = size + later * part
    kept, *sent = call(
        functools.partial(first_kernel, rows, later),
        [shape((part, vectors), BF16)] + [shape((each, width), BF16)] * rows,
        [*shares, top, rhs, off],
        scratch=[
            pltpu.VMEM((size, vectors), BF16),
            pltpu.VMEM((vectors, size), F32),
            pltpu.VMEM((later, vectors, part), F32),
        ],
        flops=4 * size * size * vectors,
    )
    messages = [over_rows(x, step) for step, x in enumerate(sent)]
    far_messages = [flip(x) for x in messages]
    bits = [1 << b for b in range(rows.bit_length() - 1)]
    blocks, steps = {}, [(0, 0)]
    for level in range(1, later):
        have = [owned[level - 1]]
        for turn in zip(bits, bits[::-1]):
            have += [over_turns(x, turn) for x in have]
        blocks[level] = have
    for turn in zip(bits, bits[::-1]):
        steps += [(even ^ turn[0], odd ^ turn[1]) for even, odd in steps]

    own, far = list(messages), list(far_messages)
    places = [None] * (2 * rows)
    turns = [(step, step) for step in range(rows)]
    past = []
    solved = []
    for level in range(1, levels):
        (weights,) = call(
            functools.partial(weights_kernel, half, level - 1, tuple(turns)),
            [shape((2 * rows, half, 8, 128), F32)],
            [targets, far_targets],
            scalars=2,
        )
        before = []
        if past:
            before = call(
                functools.partial(earlier_kernel, half, level - 1, tuple(x[0] for x in past)),
                [shape((half, each, size), F32)],
                [targets, far_targets, *(x[1] for x in past), *(x[2] for x in past)],
                scalars=2,
            )
        out = call(
            functools.partial(slots_kernel, half, tuple(places)),
            [shape((each, size), BF16)] * half,
            [weights, *own, *far, *before],
        )
        arrived = [over_pairs(x, step) for step, x in enumerate(out)]
        if level < later:
            value, products = call(
                functools.partial(middle_kernel, rows, half, level),
                [shape((each, size), BF16), shape((rows, each, size), BF16)],
                [*messages, *arrived, inverse, *blocks[level]],
                scratch=[pltpu.VMEM((each, size), F32)],
                flops=2 * each * size * size * (rows + 1),
            )
            solved.append(value)
            far_products = flip(products)
            past += list(zip([(level - 1, turn, at) for turn, at in zip(turns, places)], own, far))
            own, far, turns, places = [products] * rows, [far_products] * rows, steps, [*range(rows)] * 2
    pieces = call(
        functools.partial(last_kernel, rows, half, later, len(solved)),
        [shape((later, each, part), BF16)] * rows,
        [*messages, *arrived, inverse, *solved],
        scratch=[pltpu.VMEM((each, size), F32)],
        flops=2 * each * size * size,
    )
    pieces = [over_rows(x, step) for step, x in enumerate(pieces)]
    (out,) = call(
        functools.partial(output_kernel, rows, later),
        [shape((levels, 1, part, vectors), BF16)],
        [kept, *pieces],
        out_space=pl.ANY,
        scratch=[pltpu.VMEM((later, vectors, part), F32), pltpu.VMEM((later, part, vectors), BF16), pltpu.SemaphoreType.DMA((levels,))],
    )
    return out


def solution(mesh):
    in_specs = (
        P(None, "pcol", "prow", None),
        P(None, "pcol", None, None),
        P(None, "pcol", "prow", None, None),
        P(None, "pcol", None),
    )
    out_specs = P(None, "pcol", "prow", None)

    return jax.shard_map(local, mesh=mesh, in_specs=in_specs, out_specs=out_specs, check_vma=False)
```

```python
import functools

import jax
import jax.numpy as jnp
from jax import lax
from jax.experimental import pallas as pl
from jax.experimental.pallas import tpu as pltpu
from jax.sharding import PartitionSpec as P


F32 = jnp.float32
BF16 = jnp.bfloat16
NT = (((1,), (1,)), ((), ()))
GRANT = 24 << 20


def pairs(size, step):
    return [(i, i ^ step) for i in range(size)]


def call(kernel, out_shapes, operands, scalars=0, placed=0, out_space=pltpu.VMEM, scratch=(), flops=0):
    vmem = pl.BlockSpec(memory_space=pltpu.VMEM)
    smem = pl.BlockSpec(memory_space=pltpu.SMEM)
    moved = sum(x.size * x.dtype.itemsize for x in operands)
    return pl.pallas_call(
        kernel,
        out_shape=out_shapes,
        in_specs=[smem] * scalars + [vmem] * (len(operands) - scalars - placed) + [pl.BlockSpec(memory_space=pltpu.HBM if placed == len(operands) else pl.ANY)] * placed,
        out_specs=[pl.BlockSpec(memory_space=out_space)] * len(out_shapes),
        scratch_shapes=list(scratch),
        compiler_params=pltpu.CompilerParams(vmem_limit_bytes=GRANT),
        cost_estimate=pl.CostEstimate(flops=flops, bytes_accessed=moved, transcendentals=0),
    )(*operands)


def load_kernel(places, *refs):
    done = refs[-1]
    outs = refs[len(refs) - 1 - len(places) : -1]
    copies = [pltpu.make_async_copy(refs[at].at[place], out, done.at[i]) for i, ((at, place), out) in enumerate(zip(places, outs))]
    for copy in copies:
        copy.start()
    for copy in copies:
        copy.wait()


def first_kernel(rows, later, *refs):
    shares = refs[:rows]
    inverse, rhs, off, kept = refs[rows : rows + 4]
    messages = refs[rows + 4 : 2 * rows + 4]
    whole, turned, turned_rest = refs[2 * rows + 4 :]
    part, vectors = shares[0].shape
    size = inverse.shape[-1]
    each = vectors // rows
    me = lax.axis_index("prow")
    for step in range(rows):
        whole[pl.ds(pl.multiple_of((me ^ step) * part, part), part), :] = shares[step][...]
    solved = jnp.dot(inverse[...], whole[...], preferred_element_type=F32).astype(BF16)
    whole[...] = solved
    kept[...] = whole[pl.ds(pl.multiple_of(me * part, part), part), :]
    product = jnp.dot(off[...], solved, preferred_element_type=F32)
    turned[...] = product.T
    for level in range(later):
        turned_rest[level] = rhs[level + 1, 0].astype(F32).T
    for step in range(rows):
        at = pl.ds(pl.multiple_of((me ^ step) * each, each), each)
        messages[step][:, :size] = turned[at, :].astype(BF16)
        for level in range(later):
            low = size + level * part
            messages[step][:, low : low + part] = turned_rest[level, at, :].astype(BF16)


def slot_of(targets, source, turns, odd, half, level):
    me_col = lax.axis_index("pcol")
    turn = turns[0] if turns[0] == turns[1] else jnp.where(odd == 1, turns[1], turns[0])
    column = targets[source, 0, lax.axis_index("prow") ^ turn] - level * 2 * half
    wanted = (column >= 0) & (column < 2 * half) & ((column & 1) == (me_col & 1))
    return wanted, (column >> 1) ^ (me_col >> 1)


def weights_kernel(half, level, turns, own_targets, far_targets, out):
    parity = lax.axis_index("pcol") & 1
    for group, (targets, odd) in enumerate(((own_targets, parity), (far_targets, 1 - parity))):
        for at, turn in enumerate(turns):
            wanted, slot = slot_of(targets, level, turn, odd, half, level)
            for step in range(half):
                value = jnp.where(wanted & (slot == step), 1.0, 0.0).astype(F32)
                out[group * len(turns) + at, step] = jnp.full(out.shape[2:], value, F32)


def earlier_kernel(half, level, sources, own_targets, far_targets, *refs):
    own = refs[: len(sources)]
    far = refs[len(sources) : 2 * len(sources)]
    total = refs[-1]
    size = total.shape[2]
    parity = lax.axis_index("pcol") & 1
    total[...] = jnp.zeros_like(total)

    def add(wanted, slot, at, ref):
        @pl.when(wanted)
        def _():
            value = ref[:, :size] if at is None else ref[at]
            total[slot] += value.astype(F32)

    for targets, group, odd in ((own_targets, own, parity), (far_targets, far, 1 - parity)):
        for (source, turns, at), ref in zip(sources, group):
            add(*slot_of(targets, source, turns, odd, half, level), at, ref)


def slots_kernel(half, places, weights, *refs):
    products = refs[: len(places)]
    outs = refs[-half:]
    before = refs[len(places) : -half]
    each, size = outs[0].shape
    chunk = min(16, each)
    for low in range(0, each, chunk):
        at_rows = pl.ds(low, chunk)
        totals = [before[0][step, at_rows, :] if before else jnp.zeros((chunk, size), F32) for step in range(half)]
        for number, (at, ref) in enumerate(zip(places, products)):
            value = (ref[at_rows, :size] if at is None else ref[at, at_rows, :]).astype(F32)
            for step in range(half):
                totals[step] = totals[step] + value * jnp.tile(weights[number, step], (chunk // 8, size // 128))
        for step in range(half):
            outs[step][at_rows, :] = totals[step].astype(outs[step].dtype)


def residual(rows, level, messages, arrived, out):
    each, size = out.shape
    part = size // rows
    me = lax.axis_index("prow")
    total = arrived[0][...].astype(F32)
    for ref in arrived[1:]:
        total = total + ref[...].astype(F32)
    low = size + level * part
    if part % 128 == 0:
        for step in range(rows):
            at = pl.ds(pl.multiple_of((me ^ step) * part, part), part)
            out[:, at] = messages[step][:, low : low + part].astype(F32)
        return out[...] - total
    given = jnp.zeros((each, size), F32)
    for step in range(rows):
        place = lax.broadcasted_iota(jnp.int32, (part, size), 1) - (me ^ step) * part
        chosen = (place == lax.broadcasted_iota(jnp.int32, (part, size), 0)).astype(F32).astype(BF16)
        given = given + jnp.dot(messages[step][:, low : low + part], chosen, preferred_element_type=F32)
    return given - total


def solve(inverse, level, given):
    high = given.astype(BF16)
    low = (given - high.astype(F32)).astype(BF16)
    both = jnp.concatenate([high, low], axis=0)
    wide = lax.dot_general(both, inverse[level, 0], NT, preferred_element_type=F32)
    each = given.shape[0]
    return (wide[:each] + wide[each:]).astype(BF16)


def middle_kernel(rows, half, level, *refs):
    messages = refs[:rows]
    arrived = refs[rows : rows + half]
    inverse = refs[rows + half]
    blocks = refs[rows + half + 1 : 2 * rows + half + 1]
    solved, products, scratch = refs[2 * rows + half + 1 :]
    given = residual(rows, level - 1, messages, arrived, scratch)
    value = solve(inverse, level, given)
    solved[...] = value
    for at, block in enumerate(blocks):
        products[at] = lax.dot_general(value, block[...], NT, preferred_element_type=F32).astype(BF16)


def last_kernel(rows, half, level, before, *refs):
    messages = refs[:rows]
    arrived = refs[rows : rows + half]
    inverse = refs[rows + half]
    earlier = refs[rows + half + 1 : rows + half + 1 + before]
    outs = refs[rows + half + 1 + before : 2 * rows + half + 1 + before]
    scratch = refs[-1]
    _, size = scratch.shape
    part = size // rows
    me = lax.axis_index("prow")
    given = residual(rows, level - 1, messages, arrived, scratch)
    values = [ref[...] for ref in earlier] + [solve(inverse, level, given)]
    for index, value in enumerate(values):
        if part % 128 == 0:
            scratch[...] = value.astype(F32)
            for step in range(rows):
                at = pl.ds(pl.multiple_of((me ^ step) * part, part), part)
                outs[step][index] = scratch[:, at].astype(BF16)
        else:
            for step in range(rows):
                place = lax.broadcasted_iota(jnp.int32, (part, size), 1) - (me ^ step) * part
                chosen = (place == lax.broadcasted_iota(jnp.int32, (part, size), 0)).astype(F32).astype(BF16)
                outs[step][index] = lax.dot_general(value, chosen, NT, preferred_element_type=F32).astype(BF16)


def output_kernel(rows, later, *refs):
    kept = refs[0]
    pieces = refs[1 : rows + 1]
    out, scratch, turned, done = refs[rows + 1 :]
    _, each, _ = pieces[0].shape
    me = lax.axis_index("prow")
    copies = [pltpu.make_async_copy(kept, out.at[0, 0], done.at[0])]
    copies[0].start()
    for level in range(later):
        for step in range(rows):
            at = pl.ds(pl.multiple_of((me ^ step) * each, each), each)
            scratch[level, at, :] = pieces[step][level].astype(F32)
        turned[level] = scratch[level].T.astype(BF16)
        copies.append(pltpu.make_async_copy(turned.at[level], out.at[level + 1, 0], done.at[level + 1]))
        copies[-1].start()
    for copy in copies:
        copy.wait()


def local(rhs, inverse, off, targets):
    levels, _, part, vectors = rhs.shape
    size = inverse.shape[-1]
    rows, columns = lax.axis_size("prow"), lax.axis_size("pcol")
    half = columns // 2
    later = levels - 1
    each = vectors // rows
    shape = jax.ShapeDtypeStruct

    def over_rows(x, step):
        return lax.ppermute(x, "prow", pairs(rows, step)) if step else x

    def over_turns(x, turn):
        links = [(r * columns + c, (r ^ turn[c % 2]) * columns + c) for r in range(rows) for c in range(columns)]
        return lax.ppermute(x, ("prow", "pcol"), links)

    def over_pairs(x, step):
        return lax.ppermute(x, "pcol", pairs(columns, 2 * step)) if step else x

    def flip(x):
        return lax.ppermute(x, "pcol", pairs(columns, 1))

    far_targets = flip(targets)

    def load(places, out_shapes, operands):
        return call(
            functools.partial(load_kernel, places),
            out_shapes,
            [pltpu.with_memory_space_constraint(x, pltpu.HBM) for x in operands],
            placed=len(operands),
            scratch=[pltpu.SemaphoreType.DMA((len(places),))],
        )

    first, *owned = load(
        [(0, (0, 0))] + [(1, (level, 0, 0)) for level in range(1, later)],
        [shape((part, vectors), BF16)] + [shape((size, size), BF16)] * (later - 1),
        [rhs, off],
    )
    top, side = load([(0, (0, 0)), (1, (0, 0, 0))], [shape((size, size), BF16)] * 2, [inverse, off])
    shares = [over_rows(first, step) for step in range(rows)]
    width = size + later * part
    kept, *sent = call(
        functools.partial(first_kernel, rows, later),
        [shape((part, vectors), BF16)] + [shape((each, width), BF16)] * rows,
        [*shares, top, rhs, side],
        scratch=[
            pltpu.VMEM((size, vectors), BF16),
            pltpu.VMEM((vectors, size), F32),
            pltpu.VMEM((later, vectors, part), F32),
        ],
        flops=4 * size * size * vectors,
    )
    messages = [over_rows(x, step) for step, x in enumerate(sent)]
    far_messages = [flip(x) for x in messages]
    bits = [1 << b for b in range(rows.bit_length() - 1)]
    blocks, steps = {}, [(0, 0)]
    for level in range(1, later):
        have = [owned[level - 1]]
        for turn in zip(bits[::-1], bits):
            have += [over_turns(x, turn) for x in have]
        blocks[level] = have
    for turn in zip(bits[::-1], bits):
        steps += [(even ^ turn[0], odd ^ turn[1]) for even, odd in steps]

    own, far = list(messages), list(far_messages)
    places = [None] * (2 * rows)
    turns = [(step, step) for step in range(rows)]
    past = []
    solved = []
    for level in range(1, levels):
        (weights,) = call(
            functools.partial(weights_kernel, half, level - 1, tuple(turns)),
            [shape((2 * rows, half, 8, 128), F32)],
            [targets, far_targets],
            scalars=2,
        )
        before = []
        if past:
            before = call(
                functools.partial(earlier_kernel, half, level - 1, tuple(x[0] for x in past)),
                [shape((half, each, size), F32)],
                [targets, far_targets, *(x[1] for x in past), *(x[2] for x in past)],
                scalars=2,
            )
        out = call(
            functools.partial(slots_kernel, half, tuple(places)),
            [shape((each, size), BF16)] * half,
            [weights, *own, *far, *before],
        )
        arrived = [over_pairs(x, step) for step, x in enumerate(out)]
        if level < later:
            value, products = call(
                functools.partial(middle_kernel, rows, half, level),
                [shape((each, size), BF16), shape((rows, each, size), BF16)],
                [*messages, *arrived, inverse, *blocks[level]],
                scratch=[pltpu.VMEM((each, size), F32)],
                flops=2 * each * size * size * (rows + 1),
            )
            solved.append(value)
            far_products = flip(products)
            past += list(zip([(level - 1, turn, at) for turn, at in zip(turns, places)], own, far))
            own, far, turns, places = [products] * rows, [far_products] * rows, steps, [*range(rows)] * 2
    pieces = call(
        functools.partial(last_kernel, rows, half, later, len(solved)),
        [shape((later, each, part), BF16)] * rows,
        [*messages, *arrived, inverse, *solved],
        scratch=[pltpu.VMEM((each, size), F32)],
        flops=2 * each * size * size,
    )
    pieces = [over_rows(x, step) for step, x in enumerate(pieces)]
    (out,) = call(
        functools.partial(output_kernel, rows, later),
        [shape((levels, 1, part, vectors), BF16)],
        [kept, *pieces],
        out_space=pl.ANY,
        scratch=[pltpu.VMEM((later, vectors, part), F32), pltpu.VMEM((later, part, vectors), BF16), pltpu.SemaphoreType.DMA((levels,))],
    )
    return out


def solution(mesh):
    in_specs = (
        P(None, "pcol", "prow", None),
        P(None, "pcol", None, None),
        P(None, "pcol", "prow", None, None),
        P(None, "pcol", None),
    )
    out_specs = P(None, "pcol", "prow", None)

    return jax.shard_map(local, mesh=mesh, in_specs=in_specs, out_specs=out_specs, check_vma=False)
```

```python
import functools

import jax
import jax.numpy as jnp
from jax import lax
from jax.experimental import pallas as pl
from jax.experimental.pallas import tpu as pltpu
from jax.sharding import PartitionSpec as P


F32 = jnp.float32
BF16 = jnp.bfloat16
NT = (((1,), (1,)), ((), ()))
GRANT = 24 << 20


def pairs(size, step):
    return [(i, i ^ step) for i in range(size)]


def call(kernel, out_shapes, operands, scalars=0, placed=0, out_space=pltpu.VMEM, scratch=(), flops=0):
    vmem = pl.BlockSpec(memory_space=pltpu.VMEM)
    smem = pl.BlockSpec(memory_space=pltpu.SMEM)
    moved = sum(x.size * x.dtype.itemsize for x in operands)
    return pl.pallas_call(
        kernel,
        out_shape=out_shapes,
        in_specs=[smem] * scalars + [vmem] * (len(operands) - scalars - placed) + [pl.BlockSpec(memory_space=pltpu.HBM if placed == len(operands) else pl.ANY)] * placed,
        out_specs=[pl.BlockSpec(memory_space=out_space)] * len(out_shapes),
        scratch_shapes=list(scratch),
        compiler_params=pltpu.CompilerParams(vmem_limit_bytes=GRANT),
        cost_estimate=pl.CostEstimate(flops=flops, bytes_accessed=moved, transcendentals=0),
    )(*operands)


def load_kernel(places, *refs):
    done = refs[-1]
    outs = refs[len(refs) - 1 - len(places) : -1]
    copies = [pltpu.make_async_copy(refs[at].at[place], out, done.at[i]) for i, ((at, place), out) in enumerate(zip(places, outs))]
    for copy in copies:
        copy.start()
    for copy in copies:
        copy.wait()


def first_kernel(rows, later, *refs):
    shares = refs[:rows]
    inverse, rhs, off, kept = refs[rows : rows + 4]
    messages = refs[rows + 4 : 2 * rows + 4]
    whole, turned, turned_rest = refs[2 * rows + 4 :]
    part, vectors = shares[0].shape
    size = inverse.shape[-1]
    each = vectors // rows
    me = lax.axis_index("prow")
    for step in range(rows):
        whole[pl.ds(pl.multiple_of((me ^ step) * part, part), part), :] = shares[step][...]
    solved = jnp.dot(inverse[...], whole[...], preferred_element_type=F32).astype(BF16)
    whole[...] = solved
    kept[...] = whole[pl.ds(pl.multiple_of(me * part, part), part), :]
    product = jnp.dot(off[...], solved, preferred_element_type=F32)
    turned[...] = product.T
    for level in range(later):
        turned_rest[level] = rhs[level + 1, 0].astype(F32).T
    for step in range(rows):
        at = pl.ds(pl.multiple_of((me ^ step) * each, each), each)
        messages[step][:, :size] = turned[at, :].astype(BF16)
        for level in range(later):
            low = size + level * part
            messages[step][:, low : low + part] = turned_rest[level, at, :].astype(BF16)


def slot_of(targets, source, turns, odd, half, level):
    me_col = lax.axis_index("pcol")
    turn = turns[0] if turns[0] == turns[1] else jnp.where(odd == 1, turns[1], turns[0])
    column = targets[source, 0, lax.axis_index("prow") ^ turn] - level * 2 * half
    slot = (column >> 1) ^ (me_col >> 1)
    wanted = (column >= 0) & (column < 2 * half) & (((column ^ me_col) & 1) == jnp.where(slot == 0, 0, 1))
    return wanted, slot


def weights_kernel(half, level, turns, own_targets, far_targets, out):
    parity = lax.axis_index("pcol") & 1
    for group, (targets, odd) in enumerate(((own_targets, parity), (far_targets, 1 - parity))):
        for at, turn in enumerate(turns):
            wanted, slot = slot_of(targets, level, turn, odd, half, level)
            for step in range(half):
                value = jnp.where(wanted & (slot == step), 1.0, 0.0).astype(F32)
                out[group * len(turns) + at, step] = jnp.full(out.shape[2:], value, F32)


def earlier_kernel(half, level, sources, own_targets, far_targets, *refs):
    own = refs[: len(sources)]
    far = refs[len(sources) : 2 * len(sources)]
    total = refs[-1]
    size = total.shape[2]
    parity = lax.axis_index("pcol") & 1
    total[...] = jnp.zeros_like(total)

    def add(wanted, slot, at, ref):
        @pl.when(wanted)
        def _():
            value = ref[:, :size] if at is None else ref[at]
            total[slot] += value.astype(F32)

    for targets, group, odd in ((own_targets, own, parity), (far_targets, far, 1 - parity)):
        for (source, turns, at), ref in zip(sources, group):
            add(*slot_of(targets, source, turns, odd, half, level), at, ref)


def slots_kernel(half, places, weights, *refs):
    products = refs[: len(places)]
    outs = refs[-half:]
    before = refs[len(places) : -half]
    each, size = outs[0].shape
    chunk = min(16, each)
    for low in range(0, each, chunk):
        at_rows = pl.ds(low, chunk)
        totals = [before[0][step, at_rows, :] if before else jnp.zeros((chunk, size), F32) for step in range(half)]
        for number, (at, ref) in enumerate(zip(places, products)):
            value = (ref[at_rows, :size] if at is None else ref[at, at_rows, :]).astype(F32)
            for step in range(half):
                totals[step] = totals[step] + value * jnp.tile(weights[number, step], (chunk // 8, size // 128))
        for step in range(half):
            outs[step][at_rows, :] = totals[step].astype(outs[step].dtype)


def residual(rows, level, messages, arrived, out):
    each, size = out.shape
    part = size // rows
    me = lax.axis_index("prow")
    total = arrived[0][...].astype(F32)
    for ref in arrived[1:]:
        total = total + ref[...].astype(F32)
    low = size + level * part
    if part % 128 == 0:
        for step in range(rows):
            at = pl.ds(pl.multiple_of((me ^ step) * part, part), part)
            out[:, at] = messages[step][:, low : low + part].astype(F32)
        return out[...] - total
    given = jnp.zeros((each, size), F32)
    for step in range(rows):
        place = lax.broadcasted_iota(jnp.int32, (part, size), 1) - (me ^ step) * part
        chosen = (place == lax.broadcasted_iota(jnp.int32, (part, size), 0)).astype(F32).astype(BF16)
        given = given + jnp.dot(messages[step][:, low : low + part], chosen, preferred_element_type=F32)
    return given - total


def solve(inverse, level, given):
    high = given.astype(BF16)
    low = (given - high.astype(F32)).astype(BF16)
    both = jnp.concatenate([high, low], axis=0)
    wide = lax.dot_general(both, inverse[level, 0], NT, preferred_element_type=F32)
    each = given.shape[0]
    return (wide[:each] + wide[each:]).astype(BF16)


def middle_kernel(rows, half, level, count, *refs):
    messages = refs[:rows]
    arrived = refs[rows : rows + half]
    inverse = refs[rows + half]
    blocks = refs[rows + half + 1 : rows + half + 1 + count]
    solved, products, scratch = refs[rows + half + 1 + count :]
    given = residual(rows, level - 1, messages, arrived, scratch)
    value = solve(inverse, level, given)
    solved[...] = value
    for at, block in enumerate(blocks):
        products[at] = lax.dot_general(value, block[...], NT, preferred_element_type=F32).astype(BF16)


def relayed_kernel(solved, *refs):
    products = refs[-1]
    for at, block in enumerate(refs[:-1]):
        products[at] = lax.dot_general(solved[...], block[...], NT, preferred_element_type=F32).astype(BF16)


def last_kernel(rows, half, level, before, *refs):
    messages = refs[:rows]
    arrived = refs[rows : rows + half]
    inverse = refs[rows + half]
    earlier = refs[rows + half + 1 : rows + half + 1 + before]
    outs = refs[rows + half + 1 + before : 2 * rows + half + 1 + before]
    scratch = refs[-1]
    _, size = scratch.shape
    part = size // rows
    me = lax.axis_index("prow")
    given = residual(rows, level - 1, messages, arrived, scratch)
    values = [ref[...] for ref in earlier] + [solve(inverse, level, given)]
    for index, value in enumerate(values):
        if part % 128 == 0:
            scratch[...] = value.astype(F32)
            for step in range(rows):
                at = pl.ds(pl.multiple_of((me ^ step) * part, part), part)
                outs[step][index] = scratch[:, at].astype(BF16)
        else:
            for step in range(rows):
                place = lax.broadcasted_iota(jnp.int32, (part, size), 1) - (me ^ step) * part
                chosen = (place == lax.broadcasted_iota(jnp.int32, (part, size), 0)).astype(F32).astype(BF16)
                outs[step][index] = lax.dot_general(value, chosen, NT, preferred_element_type=F32).astype(BF16)


def output_kernel(rows, later, *refs):
    kept = refs[0]
    pieces = refs[1 : rows + 1]
    out, scratch, turned, done = refs[rows + 1 :]
    _, each, _ = pieces[0].shape
    me = lax.axis_index("prow")
    copies = [pltpu.make_async_copy(kept, out.at[0, 0], done.at[0])]
    copies[0].start()
    for level in range(later):
        for step in range(rows):
            at = pl.ds(pl.multiple_of((me ^ step) * each, each), each)
            scratch[level, at, :] = pieces[step][level].astype(F32)
        turned[level] = scratch[level].T.astype(BF16)
        copies.append(pltpu.make_async_copy(turned.at[level], out.at[level + 1, 0], done.at[level + 1]))
        copies[-1].start()
    for copy in copies:
        copy.wait()


def local(rhs, inverse, off, targets):
    levels, _, part, vectors = rhs.shape
    size = inverse.shape[-1]
    rows, columns = lax.axis_size("prow"), lax.axis_size("pcol")
    half = columns // 2
    later = levels - 1
    each = vectors // rows
    shape = jax.ShapeDtypeStruct

    def over_rows(x, step):
        return lax.ppermute(x, "prow", pairs(rows, step)) if step else x

    def over_turns(x, turn):
        links = [(r * columns + c, (r ^ turn[c % 2]) * columns + c) for r in range(rows) for c in range(columns)]
        return lax.ppermute(x, ("prow", "pcol"), links)

    def over_pairs(x, step):
        return lax.ppermute(x, "pcol", pairs(columns, 2 * step + 1)) if step else x

    def to_partners(x, step):
        links = [(r * columns + c, (r ^ step) * columns + (c ^ 1)) for r in range(rows) for c in range(columns)]
        return lax.ppermute(x, ("prow", "pcol"), links)

    def flip(x):
        return lax.ppermute(x, "pcol", pairs(columns, 1))

    far_targets = flip(targets)

    def load(places, out_shapes, operands):
        return call(
            functools.partial(load_kernel, places),
            out_shapes,
            [pltpu.with_memory_space_constraint(x, pltpu.HBM) for x in operands],
            placed=len(operands),
            scratch=[pltpu.SemaphoreType.DMA((len(places),))],
        )

    first, *owned = load(
        [(0, (0, 0))] + [(1, (level, 0, 0)) for level in range(1, later)],
        [shape((part, vectors), BF16)] + [shape((size, size), BF16)] * (later - 1),
        [rhs, off],
    )
    top, side = load([(0, (0, 0)), (1, (0, 0, 0))], [shape((size, size), BF16)] * 2, [inverse, off])
    shares = [over_rows(first, step) for step in range(rows)]
    width = size + later * part
    kept, *sent = call(
        functools.partial(first_kernel, rows, later),
        [shape((part, vectors), BF16)] + [shape((each, width), BF16)] * rows,
        [*shares, top, rhs, side],
        scratch=[
            pltpu.VMEM((size, vectors), BF16),
            pltpu.VMEM((vectors, size), F32),
            pltpu.VMEM((later, vectors, part), F32),
        ],
        flops=4 * size * size * vectors,
    )
    far_messages = [flip(sent[0])] + [to_partners(x, step) for step, x in enumerate(sent) if step]
    messages = [sent[0]] + [flip(x) for x in far_messages[1:]]
    bits = [1 << b for b in range(rows.bit_length() - 1)]
    blocks, steps = {}, [(0, 0)]
    for level in range(1, later):
        have = [owned[level - 1]]
        for turn in zip(bits, bits[::-1]):
            have += [over_turns(x, turn) for x in have]
        blocks[level] = have
    for turn in zip(bits, bits[::-1]):
        steps += [(even ^ turn[0], odd ^ turn[1]) for even, odd in steps]

    own, far = list(messages), list(far_messages)
    places = [None] * (2 * rows)
    turns = [(step, step) for step in range(rows)]
    past = []
    solved = []
    for level in range(1, levels):
        (weights,) = call(
            functools.partial(weights_kernel, half, level - 1, tuple(turns)),
            [shape((2 * rows, half, 8, 128), F32)],
            [targets, far_targets],
            scalars=2,
        )
        before = []
        if past:
            before = call(
                functools.partial(earlier_kernel, half, level - 1, tuple(x[0] for x in past)),
                [shape((half, each, size), F32)],
                [targets, far_targets, *(x[1] for x in past), *(x[2] for x in past)],
                scalars=2,
            )
        out = call(
            functools.partial(slots_kernel, half, tuple(places)),
            [shape((each, size), BF16)] * half,
            [weights, *own, *far, *before],
        )
        arrived = [over_pairs(x, step) for step, x in enumerate(out)]
        if level < later:
            count = rows // 2 + 1
            value, products = call(
                functools.partial(middle_kernel, rows, half, level, count),
                [shape((each, size), BF16), shape((count, each, size), BF16)],
                [*messages, *arrived, inverse, *blocks[level][:count]],
                scratch=[pltpu.VMEM((each, size), F32)],
                flops=2 * each * size * size * (count + 1),
            )
            (relayed,) = call(
                relayed_kernel,
                [shape((rows - count, each, size), BF16)],
                [value, *blocks[level][count:]],
                flops=2 * each * size * size * (rows - count),
            )
            solved.append(value)
            past += list(zip([(level - 1, turn, at) for turn, at in zip(turns, places)], own, far))
            own = [products] * count + [relayed] * (rows - count)
            far = [flip(products)] * count + [flip(relayed)] * (rows - count)
            turns, places = steps, [*range(count), *range(rows - count)] * 2
    pieces = call(
        functools.partial(last_kernel, rows, half, later, len(solved)),
        [shape((later, each, part), BF16)] * rows,
        [*messages, *arrived, inverse, *solved],
        scratch=[pltpu.VMEM((each, size), F32)],
        flops=2 * each * size * size,
    )
    pieces = [over_rows(x, step) for step, x in enumerate(pieces)]
    (out,) = call(
        functools.partial(output_kernel, rows, later),
        [shape((levels, 1, part, vectors), BF16)],
        [kept, *pieces],
        out_space=pl.ANY,
        scratch=[pltpu.VMEM((later, vectors, part), F32), pltpu.VMEM((later, part, vectors), BF16), pltpu.SemaphoreType.DMA((levels,))],
    )
    return out


def solution(mesh):
    in_specs = (
        P(None, "pcol", "prow", None),
        P(None, "pcol", None, None),
        P(None, "pcol", "prow", None, None),
        P(None, "pcol", None),
    )
    out_specs = P(None, "pcol", "prow", None)

    return jax.shard_map(local, mesh=mesh, in_specs=in_specs, out_specs=out_specs, check_vma=False)
```

```python
import functools

import jax
import jax.numpy as jnp
from jax import lax
from jax.experimental import pallas as pl
from jax.experimental.pallas import tpu as pltpu
from jax.sharding import PartitionSpec as P


F32 = jnp.float32
BF16 = jnp.bfloat16
NT = (((1,), (1,)), ((), ()))
GRANT = 24 << 20


def pairs(size, step):
    return [(i, i ^ step) for i in range(size)]


def call(kernel, out_shapes, operands, scalars=0, placed=0, out_space=pltpu.VMEM, scratch=(), flops=0):
    vmem = pl.BlockSpec(memory_space=pltpu.VMEM)
    smem = pl.BlockSpec(memory_space=pltpu.SMEM)
    moved = sum(x.size * x.dtype.itemsize for x in operands)
    return pl.pallas_call(
        kernel,
        out_shape=out_shapes,
        in_specs=[smem] * scalars + [vmem] * (len(operands) - scalars - placed) + [pl.BlockSpec(memory_space=pltpu.HBM if placed == len(operands) else pl.ANY)] * placed,
        out_specs=[pl.BlockSpec(memory_space=out_space)] * len(out_shapes),
        scratch_shapes=list(scratch),
        compiler_params=pltpu.CompilerParams(vmem_limit_bytes=GRANT),
        cost_estimate=pl.CostEstimate(flops=flops, bytes_accessed=moved, transcendentals=0),
    )(*operands)


def load_kernel(places, *refs):
    done = refs[-1]
    outs = refs[len(refs) - 1 - len(places) : -1]
    copies = [pltpu.make_async_copy(refs[at].at[place], out, done.at[i]) for i, ((at, place), out) in enumerate(zip(places, outs))]
    for copy in copies:
        copy.start()
    for copy in copies:
        copy.wait()


def first_kernel(rows, later, *refs):
    shares = refs[:rows]
    inverse, rhs, off, kept = refs[rows : rows + 4]
    messages = refs[rows + 4 : 2 * rows + 4]
    whole, turned, turned_rest = refs[2 * rows + 4 :]
    part, vectors = shares[0].shape
    size = inverse.shape[-1]
    each = vectors // rows
    me = lax.axis_index("prow")
    for step in range(rows):
        whole[pl.ds(pl.multiple_of((me ^ step) * part, part), part), :] = shares[step][...]
    solved = jnp.dot(inverse[...], whole[...], preferred_element_type=F32).astype(BF16)
    whole[...] = solved
    kept[...] = whole[pl.ds(pl.multiple_of(me * part, part), part), :]
    product = jnp.dot(off[...], solved, preferred_element_type=F32)
    turned[...] = product.T
    for level in range(later):
        turned_rest[level] = rhs[level + 1, 0].astype(F32).T
    for step in range(rows):
        at = pl.ds(pl.multiple_of((me ^ step) * each, each), each)
        messages[step][:, :size] = turned[at, :].astype(BF16)
        for level in range(later):
            low = size + level * part
            messages[step][:, low : low + part] = turned_rest[level, at, :].astype(BF16)


def slot_of(targets, source, turns, odd, half, level, away):
    me_col = lax.axis_index("pcol")
    turn = turns[0] if turns[0] == turns[1] else jnp.where(odd == 1, turns[1], turns[0])
    column = targets[source, 0, lax.axis_index("prow") ^ turn] - level * 2 * half
    slot = (column >> 1) ^ (me_col >> 1)
    wanted = (column >= 0) & (column < 2 * half) & (((column ^ me_col) & 1) == jnp.where(slot == 0, away, 1 - away))
    return wanted, slot


def weights_kernel(half, level, turns, away, own_targets, far_targets, out):
    parity = lax.axis_index("pcol") & 1
    for group, (targets, odd) in enumerate(((own_targets, parity), (far_targets, 1 - parity))):
        for at, turn in enumerate(turns):
            wanted, slot = slot_of(targets, level, turn, odd, half, level, away)
            for step in range(half):
                value = jnp.where(wanted & (slot == step), 1.0, 0.0).astype(F32)
                out[group * len(turns) + at, step] = jnp.full(out.shape[2:], value, F32)


def earlier_kernel(half, level, sources, away, own_targets, far_targets, *refs):
    own = refs[: len(sources)]
    far = refs[len(sources) : 2 * len(sources)]
    total = refs[-1]
    size = total.shape[2]
    parity = lax.axis_index("pcol") & 1
    total[...] = jnp.zeros_like(total)

    def add(wanted, slot, at, ref):
        @pl.when(wanted)
        def _():
            value = ref[:, :size] if at is None else ref[at]
            total[slot] += value.astype(F32)

    for targets, group, odd in ((own_targets, own, parity), (far_targets, far, 1 - parity)):
        for (source, turns, at), ref in zip(sources, group):
            add(*slot_of(targets, source, turns, odd, half, level, away), at, ref)


def slots_kernel(half, places, weights, *refs):
    products = refs[: len(places)]
    outs = refs[-half:]
    before = refs[len(places) : -half]
    each, size = outs[0].shape
    chunk = min(16, each)
    for low in range(0, each, chunk):
        at_rows = pl.ds(low, chunk)
        totals = [before[0][step, at_rows, :] if before else jnp.zeros((chunk, size), F32) for step in range(half)]
        for number, (at, ref) in enumerate(zip(places, products)):
            value = (ref[at_rows, :size] if at is None else ref[at, at_rows, :]).astype(F32)
            for step in range(half):
                totals[step] = totals[step] + value * jnp.tile(weights[number, step], (chunk // 8, size // 128))
        for step in range(half):
            outs[step][at_rows, :] = totals[step].astype(outs[step].dtype)


def residual(rows, level, messages, arrived, out):
    each, size = out.shape
    part = size // rows
    me = lax.axis_index("prow")
    total = arrived[0][...].astype(F32)
    for ref in arrived[1:]:
        total = total + ref[...].astype(F32)
    low = size + level * part
    if part % 128 == 0:
        for step in range(rows):
            at = pl.ds(pl.multiple_of((me ^ step) * part, part), part)
            out[:, at] = messages[step][:, low : low + part].astype(F32)
        return out[...] - total
    given = jnp.zeros((each, size), F32)
    for step in range(rows):
        place = lax.broadcasted_iota(jnp.int32, (part, size), 1) - (me ^ step) * part
        chosen = (place == lax.broadcasted_iota(jnp.int32, (part, size), 0)).astype(F32).astype(BF16)
        given = given + jnp.dot(messages[step][:, low : low + part], chosen, preferred_element_type=F32)
    return given - total


def solve(inverse, level, given):
    high = given.astype(BF16)
    low = (given - high.astype(F32)).astype(BF16)
    both = jnp.concatenate([high, low], axis=0)
    wide = lax.dot_general(both, inverse[level, 0], NT, preferred_element_type=F32)
    each = given.shape[0]
    return (wide[:each] + wide[each:]).astype(BF16)


def middle_kernel(rows, half, level, count, *refs):
    messages = refs[:rows]
    arrived = refs[rows : rows + half]
    inverse = refs[rows + half]
    blocks = refs[rows + half + 1 : rows + half + 1 + count]
    solved, products, scratch = refs[rows + half + 1 + count :]
    given = residual(rows, level - 1, messages, arrived, scratch)
    value = solve(inverse, level, given)
    solved[...] = value
    for at, block in enumerate(blocks):
        products[at] = lax.dot_general(value, block[...], NT, preferred_element_type=F32).astype(BF16)


def relayed_kernel(solved, *refs):
    products = refs[-1]
    for at, block in enumerate(refs[:-1]):
        products[at] = lax.dot_general(solved[...], block[...], NT, preferred_element_type=F32).astype(BF16)


def last_kernel(rows, half, level, before, *refs):
    messages = refs[:rows]
    arrived = refs[rows : rows + half]
    inverse = refs[rows + half]
    earlier = refs[rows + half + 1 : rows + half + 1 + before]
    outs = refs[rows + half + 1 + before : 2 * rows + half + 1 + before]
    scratch = refs[-1]
    _, size = scratch.shape
    part = size // rows
    me = lax.axis_index("prow")
    given = residual(rows, level - 1, messages, arrived, scratch)
    values = [ref[...] for ref in earlier] + [solve(inverse, level, given)]
    for index, value in enumerate(values):
        if part % 128 == 0:
            scratch[...] = value.astype(F32)
            for step in range(rows):
                at = pl.ds(pl.multiple_of((me ^ step) * part, part), part)
                outs[step][index] = scratch[:, at].astype(BF16)
        else:
            for step in range(rows):
                place = lax.broadcasted_iota(jnp.int32, (part, size), 1) - (me ^ step) * part
                chosen = (place == lax.broadcasted_iota(jnp.int32, (part, size), 0)).astype(F32).astype(BF16)
                outs[step][index] = lax.dot_general(value, chosen, NT, preferred_element_type=F32).astype(BF16)


def output_kernel(rows, later, *refs):
    kept = refs[0]
    pieces = refs[1 : rows + 1]
    out, scratch, turned, done = refs[rows + 1 :]
    _, each, _ = pieces[0].shape
    me = lax.axis_index("prow")
    copies = [pltpu.make_async_copy(kept, out.at[0, 0], done.at[0])]
    copies[0].start()
    for level in range(later):
        for step in range(rows):
            at = pl.ds(pl.multiple_of((me ^ step) * each, each), each)
            scratch[level, at, :] = pieces[step][level].astype(F32)
        turned[level] = scratch[level].T.astype(BF16)
        copies.append(pltpu.make_async_copy(turned.at[level], out.at[level + 1, 0], done.at[level + 1]))
        copies[-1].start()
    for copy in copies:
        copy.wait()


def local(rhs, inverse, off, targets):
    levels, _, part, vectors = rhs.shape
    size = inverse.shape[-1]
    rows, columns = lax.axis_size("prow"), lax.axis_size("pcol")
    half = columns // 2
    later = levels - 1
    each = vectors // rows
    shape = jax.ShapeDtypeStruct

    def over_rows(x, step):
        return lax.ppermute(x, "prow", pairs(rows, step)) if step else x

    def over_turns(x, turn):
        links = [(r * columns + c, (r ^ turn[c % 2]) * columns + c) for r in range(rows) for c in range(columns)]
        return lax.ppermute(x, ("prow", "pcol"), links)

    def over_pairs(x, step):
        return lax.ppermute(x, "pcol", pairs(columns, 2 * step + 1)) if step else x

    def to_partners(x, step):
        links = [(r * columns + c, (r ^ step) * columns + (c ^ 1)) for r in range(rows) for c in range(columns)]
        return lax.ppermute(x, ("prow", "pcol"), links)

    def flip(x):
        return lax.ppermute(x, "pcol", pairs(columns, 1))

    far_targets = flip(targets)
    far_inverse = flip(inverse)

    def load(places, out_shapes, operands):
        return call(
            functools.partial(load_kernel, places),
            out_shapes,
            [pltpu.with_memory_space_constraint(x, pltpu.HBM) for x in operands],
            placed=len(operands),
            scratch=[pltpu.SemaphoreType.DMA((len(places),))],
        )

    first, *owned = load(
        [(0, (0, 0))] + [(1, (level, 0, 0)) for level in range(1, later)],
        [shape((part, vectors), BF16)] + [shape((size, size), BF16)] * (later - 1),
        [rhs, off],
    )
    top, side = load([(0, (0, 0)), (1, (0, 0, 0))], [shape((size, size), BF16)] * 2, [inverse, off])
    shares = [over_rows(first, step) for step in range(rows)]
    width = size + later * part
    kept, *sent = call(
        functools.partial(first_kernel, rows, later),
        [shape((part, vectors), BF16)] + [shape((each, width), BF16)] * rows,
        [*shares, top, rhs, side],
        scratch=[
            pltpu.VMEM((size, vectors), BF16),
            pltpu.VMEM((vectors, size), F32),
            pltpu.VMEM((later, vectors, part), F32),
        ],
        flops=4 * size * size * vectors,
    )
    far_messages = [flip(sent[0])] + [to_partners(x, step) for step, x in enumerate(sent) if step]
    messages = [sent[0]] + [flip(x) for x in far_messages[1:]]
    bits = [1 << b for b in range(rows.bit_length() - 1)]
    blocks, steps = {}, [(0, 0)]
    for level in range(1, later):
        have = [owned[level - 1]]
        for turn in zip(bits, bits[::-1]):
            have += [over_turns(x, turn) for x in have]
        blocks[level] = have
    for turn in zip(bits, bits[::-1]):
        steps += [(even ^ turn[0], odd ^ turn[1]) for even, odd in steps]

    own, far = list(messages), list(far_messages)
    places = [None] * (2 * rows)
    turns = [(step, step) for step in range(rows)]
    past = []
    solved = []
    for level in range(1, levels):
        (weights,) = call(
            functools.partial(weights_kernel, half, level - 1, tuple(turns), int(level == later)),
            [shape((2 * rows, half, 8, 128), F32)],
            [targets, far_targets],
            scalars=2,
        )
        before = []
        if past:
            before = call(
                functools.partial(earlier_kernel, half, level - 1, tuple(x[0] for x in past), int(level == later)),
                [shape((half, each, size), F32)],
                [targets, far_targets, *(x[1] for x in past), *(x[2] for x in past)],
                scalars=2,
            )
        out = call(
            functools.partial(slots_kernel, half, tuple(places)),
            [shape((each, size), BF16)] * half,
            [weights, *own, *far, *before],
        )
        arrived = [over_pairs(x, step) for step, x in enumerate(out)]
        if level < later:
            count = rows // 2 + 1
            value, products = call(
                functools.partial(middle_kernel, rows, half, level, count),
                [shape((each, size), BF16), shape((count, each, size), BF16)],
                [*messages, *arrived, inverse, *blocks[level][:count]],
                scratch=[pltpu.VMEM((each, size), F32)],
                flops=2 * each * size * size * (count + 1),
            )
            (relayed,) = call(
                relayed_kernel,
                [shape((rows - count, each, size), BF16)],
                [value, *blocks[level][count:]],
                flops=2 * each * size * size * (rows - count),
            )
            solved.append(flip(value))
            past += list(zip([(level - 1, turn, at) for turn, at in zip(turns, places)], own, far))
            own = [products] * count + [relayed] * (rows - count)
            far = [flip(products)] * count + [flip(relayed)] * (rows - count)
            turns, places = steps, [*range(count), *range(rows - count)] * 2
    pieces = call(
        functools.partial(last_kernel, rows, half, later, len(solved)),
        [shape((later, each, part), BF16)] * rows,
        [*far_messages, *arrived, far_inverse, *solved],
        scratch=[pltpu.VMEM((each, size), F32)],
        flops=2 * each * size * size,
    )
    pieces = [to_partners(x, step) if step else flip(x) for step, x in enumerate(pieces)]
    (out,) = call(
        functools.partial(output_kernel, rows, later),
        [shape((levels, 1, part, vectors), BF16)],
        [kept, *pieces],
        out_space=pl.ANY,
        scratch=[pltpu.VMEM((later, vectors, part), F32), pltpu.VMEM((later, part, vectors), BF16), pltpu.SemaphoreType.DMA((levels,))],
    )
    return out


def solution(mesh):
    in_specs = (
        P(None, "pcol", "prow", None),
        P(None, "pcol", None, None),
        P(None, "pcol", "prow", None, None),
        P(None, "pcol", None),
    )
    out_specs = P(None, "pcol", "prow", None)

    return jax.shard_map(local, mesh=mesh, in_specs=in_specs, out_specs=out_specs, check_vma=False)
```
